256 devices in a mesh: gx: 8 (over z_lo, core), gy: 16 (over x, y), gz: 2 (over z_hi).
Axes of the slice: x: 4, y: 4, z: 8 (z_hi: 2, z_lo: 4; z = z_hi * 4 + z_lo), core: 2. Of those that a mesh axis runs over, the one named last changes fastest.
Arguments:
- displacement: float32 [3, 256, 512, 512], P(None, 'gx', 'gy', 'gz'), may hold values from -0.0018 to 0.0018
- applied_strain: float32 [6], replicated, may hold values from -0.0003 to 0.0003
- labels: int32 [256, 512, 512], P('gx', 'gy', 'gz'), may hold values from 0 to 3
- history: float32 [256, 512, 512], P('gx', 'gy', 'gz'), may hold values from 5e-05 to 0.0006
- modulus: float32 [4], replicated, may hold values from 5000 to 60000
- poisson: float32 [4], replicated, may hold values from 0.1 to 0.3
- threshold: float32 [4], replicated, may hold values from 4e-05 to 0.00016
- ductility: float32 [4], replicated, may hold values from 0.6 to 1
- brittleness: float32 [4], replicated, may hold values from 5000 to 20000
- weight: float32 [4], replicated, may hold values from 0.1 to 1
Outputs:
- damage: float32 [256, 512, 512], P('gx', 'gy', 'gz')
- mises: float32 [256, 512, 512], P('gx', 'gy', 'gz')
The draws below stay inside these ranges and needn't reach their ends.
All inputs are finite; a program needn't handle non-finite values.
Results may differ from the reference program's by a relative error of at most 0.0003.
Values sent between devices are 32-bit elements; how exact they have to be, the bound alone decides.
No kernel may reach another device: no remote copies, remote signals or barrier semaphores. Data moves between devices by JAX's collectives and lax.ppermute only.
A program may use at most 64 MiB of HBM per device.

```python
import math
import jax
import jax.numpy as jnp

RADIUS = 8
PHASES = 4
NX = 256
NY = 512
NZ = 512


def touch_ends(entries, stream_key, low, top_value):
    index_at = [jax.random.randint(jax.random.fold_in(stream_key, axis), (), 0, length) for axis, length in enumerate(entries.shape)]
    longest = entries.shape.index(max(entries.shape))
    next_to = index_at[:longest] + [(index_at[longest] + 1) % entries.shape[longest]] + index_at[longest + 1:]
    return entries.at[tuple(index_at)].set(low).at[tuple(next_to)].set(top_value)


def block_levels(stream_key, extent, split, low, largest):
    def one(axis_at, parts):
        draws = jax.random.uniform(jax.random.fold_in(jax.random.fold_in(stream_key, 6), axis_at), (parts,), jnp.float32, low / len(split), largest / len(split))
        return jnp.repeat(jnp.exp(draws), extent[axis_at] // parts).reshape((-1,) + (1,) * (len(extent) - axis_at - 1))

    level = one(*split[0])
    for cut in split[1:]:
        level = level * one(*cut)
    return level


def centred(stream_key, dims, deviation, reach, cuts=(), held_as=jnp.bfloat16):
    values = deviation * jax.random.normal(stream_key, dims, jnp.float32)
    if cuts:
        values = values * block_levels(stream_key, dims, cuts, -0.22, 0.18)
    return jnp.clip(values, -reach, reach).astype(held_as)


def setup_inputs(seed: int = 0) -> dict:
    keys = jax.random.split(jax.random.key(seed), 11)
    return {
        "displacement": centred(keys[0], (3, NX, NY, NZ), 0.0003, 0.0018, ((1, 8), (2, 16), (3, 2)), jnp.float32),
        "applied_strain": centred(keys[1], (6,), 0.0001, 0.0003, (), jnp.float32),
        "labels": touch_ends(jax.random.randint(keys[2], (NX, NY, NZ), 0, PHASES), jax.random.fold_in(keys[2], 1), 0, PHASES - 1).astype(jnp.int32),
        "history": jnp.clip(jnp.exp(math.log(0.0006) - 2.4849067 * jax.random.uniform(keys[3], (NX, NY, NZ), jnp.float32) ** block_levels(keys[3], (NX, NY, NZ), ((0, 8), (1, 16), (2, 2)), -0.2, 0.2)), 4.999999873689376e-05, 0.0006),
        "modulus": jnp.clip(jnp.exp(jax.random.uniform(keys[4], (PHASES,), jnp.float32, math.log(5000.0), math.log(60000.0))), 5000.0, 60000.0),
        "poisson": jnp.clip(jax.random.uniform(keys[5], (PHASES,), jnp.float32, 0.1, 0.3), 0.1, 0.3),
        "threshold": jnp.clip(jnp.exp(jax.random.uniform(keys[6], (PHASES,), jnp.float32, math.log(3.9999998989515007e-05), math.log(0.00016))), 3.9999998989515007e-05, 0.00016),
        "ductility": jnp.clip(jax.random.uniform(keys[7], (PHASES,), jnp.float32, 0.6, 1.0), 0.6, 1.0),
        "brittleness": jnp.clip(jnp.exp(jax.random.uniform(keys[8], (PHASES,), jnp.float32, math.log(5000.0), math.log(20000.0))), 5000.0, 20000.0),
        "weight": jnp.clip(jnp.exp(jax.random.uniform(keys[9], (PHASES,), jnp.float32, math.log(0.1), math.log(1.0))), 0.1, 1.0),
    }


def pick_phase(labels, table):
    picked = jnp.zeros(labels.shape, table.dtype)
    for which_phase in range(table.shape[0]):
        picked = jnp.where(labels == which_phase, table[which_phase], picked)
    return picked

def difference(field, along, others):
    result = jnp.roll(field, -1, along) - field
    for other in others:
        result = result + jnp.roll(result, -1, other)
    return 0.25 * result

def invariants(grad_x, grad_y, grad_z, applied_strain):
    strain_xx = applied_strain[0] + grad_x[0]
    strain_yy = applied_strain[1] + grad_y[1]
    strain_zz = applied_strain[2] + grad_z[2]
    strain_yz = applied_strain[3] + 0.5 * (grad_y[2] + grad_z[1])
    strain_xz = applied_strain[4] + 0.5 * (grad_x[2] + grad_z[0])
    strain_xy = applied_strain[5] + 0.5 * (grad_x[1] + grad_y[0])
    trace_strain = strain_xx + strain_yy + strain_zz
    second_inv = ((strain_xx - strain_yy) ** 2 + (strain_yy - strain_zz) ** 2 + (strain_zz - strain_xx) ** 2) / 6.0
    second_inv = second_inv + strain_yz * strain_yz + strain_xz * strain_xz + strain_xy * strain_xy
    return (trace_strain, second_inv)

def equivalent(trace_strain, second_inv, ratio_nu):
    ratio = 10.0
    lateral = (ratio - 1.0) / (1.0 - 2.0 * ratio_nu)
    under = lateral * lateral * trace_strain * trace_strain + 12.0 * ratio * second_inv / (1.0 + ratio_nu) ** 2
    return (lateral * trace_strain + jnp.sqrt(under)) / (2.0 * ratio)

def smooth_periodic(field, axis):
    total = None
    for offset in range(-RADIUS, RADIUS + 1):
        coeff = math.exp(-2.0 * offset * offset / (RADIUS * RADIUS))
        term = coeff * jnp.roll(field, -offset, axis)
        total = term if total is None else total + term
    return total

def finish(averaged, history, second_inv, labels, ratio_nu, modulus, threshold, ductility, brittleness):
    kappa = jnp.maximum(history, averaged)
    start = pick_phase(labels, threshold)
    ductile = pick_phase(labels, ductility)
    brittle = pick_phase(labels, brittleness)
    grown = 1.0 - start * (1.0 - ductile) / jnp.maximum(kappa, start) - ductile * jnp.exp(-brittle * (kappa - start))
    damage = jnp.where(kappa > start, grown, 0.0)
    stiff = pick_phase(labels, modulus)
    mises = (1.0 - damage) * stiff / (1.0 + ratio_nu) * jnp.sqrt(3.0 * second_inv)
    return (damage, mises)

def reference(displacement, applied_strain, labels, history, modulus, poisson, threshold, ductility, brittleness, weight):
    grad_x = difference(displacement, 1, (2, 3))
    grad_y = difference(displacement, 2, (1, 3))
    grad_z = difference(displacement, 3, (1, 2))
    trace_strain, second_inv = invariants(grad_x, grad_y, grad_z, applied_strain)
    ratio_nu = pick_phase(labels, poisson)
    equiv_strain = equivalent(trace_strain, second_inv, ratio_nu)
    weights_field = pick_phase(labels, weight)
    upper = weights_field * equiv_strain
    lower = weights_field
    for axis in range(3):
        upper = smooth_periodic(upper, axis)
        lower = smooth_periodic(lower, axis)
    averaged = upper / lower
    return finish(averaged, history, second_inv, labels, ratio_nu, modulus, threshold, ductility, brittleness)
```

```python
import math

import jax
import jax.numpy as jnp
import numpy as np
from jax import lax
from jax.experimental import pallas as pl
from jax.experimental.pallas import tpu as pltpu
from jax.sharding import PartitionSpec as P

RADIUS = 8
F32 = jnp.float32
BF16 = jnp.bfloat16


def taps():
    return [math.exp(-2.0 * s * s / (RADIUS * RADIUS)) for s in range(-RADIUS, RADIUS + 1)]


def band(outs, ins, offset):
    table = taps()
    full = np.zeros((outs, ins), np.float64)
    for i in range(outs):
        for k in range(ins):
            s = k + offset - i
            if abs(s) <= RADIUS:
                full[i, k] = table[s + RADIUS]
    return full


def split_const(full):
    hi = full.astype(jnp.bfloat16)
    lo = (full - hi.astype(np.float64)).astype(jnp.bfloat16)
    return hi, lo


def split(f):
    hi = f.astype(BF16)
    lo = (f - hi.astype(F32)).astype(BF16)
    return hi, lo


def mxu(a, b, dims):
    return lax.dot_general(a, b, (dims, ((), ())), preferred_element_type=F32)


def shift_route(block, axes, steps):
    sizes = [lax.axis_size(a) for a in axes]
    total = math.prod(sizes)
    route = []
    for flat in range(total):
        place = np.unravel_index(flat, sizes)
        target = tuple((i + s) % n for i, s, n in zip(place, steps, sizes))
        route.append((flat, int(np.ravel_multi_index(target, sizes))))
    return lax.ppermute(block, axes if len(axes) > 1 else axes[0], route)


def swap_route(block, axis, parity):
    size = lax.axis_size(axis)
    route = []
    for k in range(0, size, 2):
        a, b = (k + parity) % size, (k + 1 + parity) % size
        route += [(a, b), (b, a)]
    return lax.ppermute(block, axis, route)


def call(kernel, outs, scratch=(), scalars=0, n_in=1, name=None, smem=()):
    specs = [
        pl.BlockSpec(memory_space=pltpu.SMEM if i in smem else pltpu.VMEM) for i in range(n_in)
    ]
    return pl.pallas_call(
        kernel,
        out_shape=[jax.ShapeDtypeStruct(s, F32) for s in outs],
        in_specs=specs,
        out_specs=[pl.BlockSpec(memory_space=pltpu.VMEM) for _ in outs],
        scratch_shapes=list(scratch),
        name=name,
    )


def pick(labels, table, row):
    out = jnp.where(labels == 0, table[row, 0], table[row, 3])
    out = jnp.where(labels == 1, table[row, 1], out)
    return jnp.where(labels == 2, table[row, 2], out)


def edge_columns(field, out_ref):
    row = lax.broadcasted_iota(jnp.int32, (16, 256), 0)
    lane = lax.broadcasted_iota(jnp.int32, (16, 256), 1)
    wanted = jnp.where(row < 8, 248 + row, row - 8)
    onehot = (lane == wanted).astype(F32)
    out_ref[...] = lax.dot_general(
        onehot, field, (((1,), (1,)), ((), ())), precision=lax.Precision.HIGHEST,
        preferred_element_type=F32,
    )


def pack_kernel(table, u, labels, ucol, wcol, wscr):
    lane = lax.broadcasted_iota(jnp.int32, (32, 128), 1)

    def step(x, cols):
        wscr[pl.ds(pl.multiple_of(x * 32, 32), 32), :] = pick(labels[x], table, 2)
        return tuple(
            jnp.where(lane == x, pltpu.roll(u[c, x, :, 0:128], x, 1), cols[c]) for c in range(3)
        )

    cols = lax.fori_loop(0, 32, step, tuple(jnp.zeros((32, 128), F32) for _ in range(3)))
    for c in range(3):
        ucol[c] = cols[c]
    edge_columns(wscr[...], wcol)


def planes_kernel(u, zt, xm, ym, xym):
    for c in range(3):
        xm[c, :, 0:256] = u[c, 0]
        xm[c, :, 256:384] = zt[c]
        for x in range(32):
            ym[c, x : x + 1, :] = u[c, x, 0:1, :]
        ym[c, 32:33, 0:128] = zt[c, 0:1, :]
        xym[c : c + 1, :] = u[c, 0, 0:1, :]
        xym[3 + c : 4 + c, 0:128] = zt[c, 0:1, :]


def combine(d, s, dsh, ssh):
    a = [d[c] + dsh[c] for c in range(3)]
    b = [ssh[c] - s[c] for c in range(3)]
    m = [ssh[c] + s[c] for c in range(3)]
    plus = [a[0], b[1], a[1] + b[0], m[2], b[2] + m[1], a[2] + m[0]]
    minus = [a[0], b[1], a[1] + b[0], m[2], b[2] - m[1], a[2] - m[0]]
    return plus, minus


def strain_kernel(table, applied, u, zt, xm, ym, xym, labels, top, stress, cols, zq):
    lane = lax.broadcasted_iota(jnp.int32, (32, 128), 1)
    lane1 = lax.broadcasted_iota(jnp.int32, (1, 128), 1)
    row_s = lax.broadcasted_iota(jnp.int32, (32, 128), 0)
    row = lax.broadcasted_iota(jnp.int32, (32, 256), 0)
    d, s, dsh, ssh = [], [], [], []
    for c in range(3):
        n = jnp.where(lane == 32, pltpu.roll(xm[c, :, 256:384], 32, 1), zt[c])
        r = jnp.where(lane1 == 32, pltpu.roll(xym[3 + c : 4 + c, 0:128], 32, 1), ym[c, 32:33, 0:128])
        nx, rx = pltpu.roll(n, 127, 1), pltpu.roll(r, 127, 1)
        d.append(nx - n)
        s.append(nx + n)
        dsh.append(jnp.where(row_s == 31, rx - r, pltpu.roll(d[c], 31, 0)))
        ssh.append(jnp.where(row_s == 31, rx + r, pltpu.roll(s[c], 31, 0)))
    plus, _ = combine(d, s, dsh, ssh)
    for q in range(6):
        zq[q] = plus[q]

    def cells(x, here, there, r_here, r_there):
        d, s, dsh, ssh = [], [], [], []
        for c in range(3):
            d.append(there[c] - here[c])
            s.append(there[c] + here[c])
            dsh.append(jnp.where(row == 31, r_there[c] - r_here[c], pltpu.roll(d[c], 31, 0)))
            ssh.append(jnp.where(row == 31, r_there[c] + r_here[c], pltpu.roll(s[c], 31, 0)))
        plus, minus = combine(d, s, dsh, ssh)
        shifted = []
        for q in range(6):
            rolled = pltpu.roll(plus[q], 255, 1)
            last = pltpu.roll(zq[q], 127 - x, 1)
            shifted.append(
                jnp.concatenate(
                    [rolled[:, 0:128], jnp.where(lane == 127, last, rolled[:, 128:256])], axis=1
                )
            )
        xx = applied[0] + 0.25 * (minus[0] + shifted[0])
        yy = applied[1] + 0.25 * (minus[1] + shifted[1])
        zz = applied[2] + 0.25 * (shifted[3] - minus[3])
        xy = applied[5] + 0.125 * (minus[2] + shifted[2])
        yz = applied[3] + 0.125 * (minus[4] + shifted[4])
        xz = applied[4] + 0.125 * (minus[5] + shifted[5])
        trace = xx + yy + zz
        p, q, r = xx - yy, yy - zz, zz - xx
        second = (p * p + q * q + r * r) * (1.0 / 6.0) + (yz * yz + xz * xz + xy * xy)
        lab = labels[x]
        lead = pick(lab, table, 0) * trace
        value = lead + jnp.sqrt(lead * lead + pick(lab, table, 1) * second)
        top[x] = value
        stress[x] = pick(lab, table, 3) * jnp.sqrt(second)

    def step(x, carry):
        cells(
            x,
            [u[c, x] for c in range(3)],
            [u[c, x + 1] for c in range(3)],
            [ym[c, pl.ds(x, 1), :] for c in range(3)],
            [ym[c, pl.ds(x + 1, 1), :] for c in range(3)],
        )
        return carry

    lax.fori_loop(0, 31, step, 0)
    cells(
        31,
        [u[c, 31] for c in range(3)],
        [xm[c, :, 0:256] for c in range(3)],
        [ym[c, 31:32, :] for c in range(3)],
        [xym[c : c + 1, :] for c in range(3)],
    )
    edge_columns(top[...].reshape(1024, 256), cols)


def smooth_z(field, halo, gz, gh):
    hi, lo = split(field)
    out = mxu(hi, gz[0], ((1,), (0,))) + mxu(lo, gz[0], ((1,), (0,))) + mxu(hi, gz[1], ((1,), (0,)))
    chi, clo = split(halo)
    c = jnp.concatenate([chi, clo, chi], axis=0)
    return out + mxu(c, gh[...], ((0,), (0,)))


def weights_z_kernel(table, odd, labels, halo, gz, gh, out, near, far):
    def step(x, carry):
        out[x] = pick(labels[x], table, 2)
        return carry

    lax.fori_loop(0, 32, step, 0)
    z_body(odd, out, halo, gz, gh, out, near, far)


def z_kernel(odd, field, halo, gz, gh, out, near, far):
    z_body(odd, field, halo, gz, gh, out, near, far)


def z_body(odd, field, halo, gz, gh, out, near, far):
    out[...] = smooth_z(field[...].reshape(1024, 256), halo[...], gz, gh).reshape(32, 32, 256)
    start = 24 * (1 - odd[0])
    near[...] = out[pl.ds(start, 8)]
    far[...] = out[pl.ds(24 - start, 8)]


def x_kernel(odd, field, r_near, r_far, out, near, far):
    is_odd = odd[0] == 1
    table = taps()

    def step(k, carry):
        rows = pl.ds(pl.multiple_of((k // 2) * 8, 8), 8)
        lanes = pl.ds(pl.multiple_of((k % 2) * 128, 128), 128)
        low, high = [], []
        for i in range(8):
            a, b = r_near[i, rows, lanes], r_far[i, rows, lanes]
            low.append(jnp.where(is_odd, a, b))
            high.append(jnp.where(is_odd, b, a))
        cells = low + [field[i, rows, lanes] for i in range(32)] + high
        for i in range(32):
            total = table[8] * cells[i + 8]
            for s in range(1, 9):
                total = total + table[8 + s] * (cells[i + 8 - s] + cells[i + 8 + s])
            out[i, rows, lanes] = total
        return carry

    lax.fori_loop(0, 8, step, 0)
    start = pl.multiple_of(24 * (1 - odd[1]), 8)
    near[...] = out[:, pl.ds(start, 8), :]
    far[...] = out[:, pl.ds(pl.multiple_of(24 - start, 8), 8), :]


def smooth_y(x, is_odd, field, r_near, r_far, gy):
    a, b = r_near[x], r_far[x]
    cells = jnp.concatenate([jnp.where(is_odd, a, b), field[x], jnp.where(is_odd, b, a)], axis=0)
    hi, lo = split(cells)
    return mxu(gy[...], jnp.concatenate([hi, lo, hi], axis=0), ((1,), (0,)))


def y_kernel(odd, field, r_near, r_far, gy, out):
    is_odd = odd[1] == 1

    def step(x, carry):
        out[x] = smooth_y(x, is_odd, field, r_near, r_far, gy)
        return carry

    lax.fori_loop(0, 32, step, 0)


def finish_kernel(
    table, odd, field, r_near, r_far, gy, bottom, history, stress, labels, damage, mises
):
    is_odd = odd[1] == 1

    def step(x, carry):
        averaged = smooth_y(x, is_odd, field, r_near, r_far, gy) / bottom[x]
        kappa = jnp.maximum(history[x], averaged)
        lab = labels[x]
        start = pick(lab, table, 4)
        grown = (
            1.0
            - pick(lab, table, 5) / jnp.maximum(kappa, start)
            - pick(lab, table, 6) * jnp.exp(pick(lab, table, 7) * (start - kappa))
        )
        harm = jnp.where(kappa > start, grown, 0.0)
        damage[x] = harm
        mises[x] = (1.0 - harm) * stress[x]
        return carry

    lax.fori_loop(0, 32, step, 0)


def shards(
    displacement,
    applied_strain,
    labels,
    history,
    modulus,
    poisson,
    threshold,
    ductility,
    brittleness,
    weight,
):
    lateral = (9.0 / 20.0) / (1.0 - 2.0 * poisson)
    table = jnp.stack(
        [
            weight * lateral,
            weight * weight * (0.3 / (1.0 + poisson) ** 2),
            weight,
            modulus / (1.0 + poisson) * math.sqrt(3.0),
            threshold,
            threshold * (1.0 - ductility),
            ductility,
            brittleness,
        ]
    )
    odd = jnp.stack([lax.axis_index("gx") % 2, lax.axis_index("gy") % 2]).astype(jnp.int32)
    gz = jnp.stack([jnp.asarray(m) for m in split_const(band(256, 256, 0).T)])
    low, high = band(256, 8, -8).T, band(256, 8, 256).T
    h_hi, h_lo = split_const(np.concatenate([low, high], axis=0))
    gh = jnp.asarray(np.concatenate([h_hi, h_hi, h_lo], axis=0))
    y_hi, y_lo = split_const(band(32, 48, -8))
    gy = jnp.asarray(np.concatenate([y_hi, y_hi, y_lo], axis=1))

    ucol, wcol = call(
        pack_kernel,
        [(3, 32, 128), (16, 1024)],
        scratch=[pltpu.VMEM((1024, 256), F32)],
        n_in=3,
        smem=(0,),
        name="pack",
    )(table, displacement, labels)
    message = jnp.concatenate([ucol.reshape(96, 128), wcol.reshape(128, 128)], axis=0)
    arrived = shift_route(message, ("gz",), (1,))
    zt, w_halo = arrived[:96].reshape(3, 32, 128), arrived[96:].reshape(16, 1024)
    xm, ym, xym = call(
        planes_kernel, [(3, 32, 384), (3, 40, 256), (8, 256)], n_in=2, name="planes"
    )(displacement, zt)
    xm = shift_route(xm, ("gx",), (-1,))
    ym = shift_route(ym, ("gy",), (-1,))
    xym = shift_route(xym, ("gx", "gy"), (-1, -1))
    field3, edge_x, edge_y = (32, 32, 256), (8, 32, 256), (32, 8, 256)
    wz, near, far = call(
        weights_z_kernel, [field3, edge_x, edge_x], n_in=6, smem=(0, 1), name="weights_z"
    )(table, odd, labels, w_halo, gz, gh)
    w_near, w_far = swap_route(near, "gx", 0), swap_route(far, "gx", 1)
    top, stress, cols = call(
        strain_kernel,
        [field3, field3, (16, 1024)],
        scratch=[pltpu.VMEM((6, 32, 128), F32)],
        n_in=8,
        smem=(0, 1),
        name="strain",
    )(table, applied_strain, displacement, zt, xm, ym, xym, labels)
    t_halo = shift_route(cols, ("gz",), (1,))
    x_call = call(x_kernel, [field3, edge_y, edge_y], n_in=4, smem=(0,), name="smooth_x")
    wx, near, far = x_call(odd, wz, w_near, w_far)
    w_near, w_far = swap_route(near, "gy", 0), swap_route(far, "gy", 1)
    tz, near, far = call(z_kernel, [field3, edge_x, edge_x], n_in=5, smem=(0,), name="top_z")(
        odd, top, t_halo, gz, gh
    )
    t_near, t_far = swap_route(near, "gx", 0), swap_route(far, "gx", 1)
    (bottom,) = call(y_kernel, [field3], n_in=5, smem=(0,), name="weights_y")(
        odd, wx, w_near, w_far, gy
    )
    tx, near, far = x_call(odd, tz, t_near, t_far)
    t_near, t_far = swap_route(near, "gy", 0), swap_route(far, "gy", 1)
    return call(finish_kernel, [field3, field3], n_in=10, smem=(0, 1), name="finish")(
        table, odd, tx, t_near, t_far, gy, bottom, history, stress, labels
    )


def solution(mesh):
    cells = P("gx", "gy", "gz")
    placed = (P(None, "gx", "gy", "gz"), P(), cells, cells, P(), P(), P(), P(), P(), P())
    return jax.shard_map(
        lambda *args: tuple(shards(*args)),
        mesh=mesh,
        in_specs=placed,
        out_specs=(cells, cells),
        check_vma=False,
    )
```

```python
import math

import jax
import jax.numpy as jnp
import numpy as np
from jax import lax
from jax.experimental import pallas as pl
from jax.experimental.pallas import tpu as pltpu
from jax.sharding import PartitionSpec as P


RADIUS = 8
F32 = jnp.float32
BF16 = jnp.bfloat16


def taps():
    return [math.exp(-2.0 * s * s / (RADIUS * RADIUS)) for s in range(-RADIUS, RADIUS + 1)]


def band(outs, ins, offset):
    table = taps()
    full = np.zeros((outs, ins), np.float64)
    for i in range(outs):
        for k in range(ins):
            s = k + offset - i
            if abs(s) <= RADIUS:
                full[i, k] = table[s + RADIUS]
    return full


def split_const(full):
    hi = full.astype(jnp.bfloat16)
    lo = (full - hi.astype(np.float64)).astype(jnp.bfloat16)
    return hi, lo


def split(f):
    hi = f.astype(BF16)
    lo = (f - hi.astype(F32)).astype(BF16)
    return hi, lo


def mxu(a, b, dims):
    return lax.dot_general(a, b, (dims, ((), ())), preferred_element_type=F32)


def shift_route(block, axes, steps):
    sizes = [lax.axis_size(a) for a in axes]
    total = math.prod(sizes)
    route = []
    for flat in range(total):
        place = np.unravel_index(flat, sizes)
        target = tuple((i + s) % n for i, s, n in zip(place, steps, sizes))
        route.append((flat, int(np.ravel_multi_index(target, sizes))))
    return lax.ppermute(block, axes if len(axes) > 1 else axes[0], route)


def swap_route(block, axis, parity):
    size = lax.axis_size(axis)
    route = []
    for k in range(0, size, 2):
        a, b = (k + parity) % size, (k + 1 + parity) % size
        route += [(a, b), (b, a)]
    return lax.ppermute(block, axis, route)


def call(
    kernel, outs, scratch=(), n_in=1, smem=(), limit=10 << 20, spaces=None, out_spaces=None,
    aliases=None, after=(), odd=None,
):
    spaces = (spaces or [None] * n_in) + [pl.ANY] * len(after)
    n_in = len(spaces) - len(after)

    def body(*refs):
        refs = [*refs[:n_in], *refs[n_in + len(after) :]]
        if odd is not None:
            refs.insert(odd, (lax.axis_index("gx") % 2, lax.axis_index("gy") % 2))
        kernel(*refs)

    specs = [
        pl.BlockSpec(memory_space=pltpu.SMEM if i in smem else space or pltpu.VMEM)
        for i, space in enumerate(spaces)
    ]
    built = pl.pallas_call(
        body,
        out_shape=[jax.ShapeDtypeStruct(s, F32) for s in outs],
        in_specs=specs,
        out_specs=[pl.BlockSpec(memory_space=s) for s in out_spaces or [pltpu.VMEM] * len(outs)],
        scratch_shapes=list(scratch),
        input_output_aliases=aliases or {},
        compiler_params=pltpu.CompilerParams(vmem_limit_bytes=limit),
    )
    return lambda *args: built(*args, *after)


def pick(labels, table, row):
    out = jnp.where(labels == 0, table[row, 0], table[row, 3])
    out = jnp.where(labels == 1, table[row, 1], out)
    return jnp.where(labels == 2, table[row, 2], out)


def edge_columns(field, put):
    for j in range(8):
        put(j, field(j, 0).T[0:8], field(j, 1).T[120:128])


def table_kernel(modulus, poisson, threshold, ductility, brittleness, weight, table):
    for k in range(4):
        nu, w = poisson[k], weight[k]
        lead, shear = 1.0 - 2.0 * nu, 1.0 / (1.0 + nu)
        table[0, k] = 0.45 * w / lead
        table[1, k] = 0.3 * (w * shear) * (w * shear)
        table[2, k] = w
        table[3, k] = math.sqrt(3.0) * modulus[k] * shear
        table[4, k] = threshold[k]
        table[5, k] = threshold[k] * (1.0 - ductility[k])
        table[6, k] = ductility[k]
        table[7, k] = brittleness[k]


def planes_kernel(u, xm, ym, kept, sem):
    keep = pltpu.make_async_copy(u, kept, sem.at[0])
    keep.start()
    for c in range(3):
        xm[c] = u[c, 0]
        for x in range(32):
            ym[c, x : x + 1, :] = u[c, x, 0:1, :]
    keep.wait()


def extend_kernel(ym, xm, out):
    for c in range(3):
        out[c, 0:32] = ym[c]
        out[c, 32:33, :] = xm[c, 0:1, :]


def weight_edges_kernel(weight, odd, labels, near, far, low, high, sem):
    copies = [
        pltpu.make_async_copy(labels.at[pl.ds(0, 8)], low, sem.at[0]),
        pltpu.make_async_copy(labels.at[pl.ds(24, 8)], high, sem.at[1]),
    ]
    for copy in copies:
        copy.start()
    for copy in copies:
        copy.wait()
    is_odd = odd[0] == 1

    def choose(lab):
        w = jnp.where(lab == 0, weight[0], weight[3])
        w = jnp.where(lab == 1, weight[1], w)
        return jnp.where(lab == 2, weight[2], w)

    def step(i, carry):
        a, b = choose(low[i]), choose(high[i])
        near[i] = jnp.where(is_odd, a, b)
        far[i] = jnp.where(is_odd, b, a)
        return carry

    lax.fori_loop(0, 8, step, 0, unroll=2)


def columns_kernel(u, labels, nodes):
    lane = lax.broadcasted_iota(jnp.int32, (32, 128), 1)

    def step(x, carry):
        first, last, lab = carry
        for c in range(3):
            at = 40 * c + x
            first = jnp.where(lane == at, pltpu.roll(u[c, x, :, 0:128], at, 1), first)
            last = jnp.where(lane == at, pltpu.roll(u[c, x, :, 128:256], at + 1, 1), last)
        moved = pltpu.roll(labels[x, :, 128:256], x + 1, 1)
        return first, last, jnp.where(lane == x, moved, lab)

    zero = jnp.zeros((32, 128), F32)
    first, last, lab = lax.fori_loop(
        0, 32, step, (zero, zero, jnp.zeros((32, 128), jnp.int32)), unroll=2
    )
    nodes[0:32, :] = first
    nodes[32:64, :] = last
    nodes[64:96, :] = lab.astype(F32)


def combine(d, s, dsh, ssh):
    a = [d[c] + dsh[c] for c in range(3)]
    b = [ssh[c] - s[c] for c in range(3)]
    m = [ssh[c] + s[c] for c in range(3)]
    plus = [a[0], b[1], a[1] + b[0], m[2], b[2] + m[1], a[2] + m[0]]
    minus = [a[0], b[1], a[1] + b[0], m[2], b[2] - m[1], a[2] - m[0]]
    return plus, minus


def respond(applied, table, lab, sums):
    xx = applied[0] + 0.25 * sums[0]
    yy = applied[1] + 0.25 * sums[1]
    zz = applied[2] + 0.25 * sums[2]
    xy = applied[5] + 0.125 * sums[3]
    yz = applied[3] + 0.125 * sums[4]
    xz = applied[4] + 0.125 * sums[5]
    trace = xx + yy + zz
    p, q, r = xx - yy, yy - zz, zz - xx
    second = (p * p + q * q + r * r) * (1.0 / 6.0) + (yz * yz + xz * xz + xy * xy)
    lead = pick(lab, table, 0) * trace
    value = lead + jnp.sqrt(lead * lead + pick(lab, table, 1) * second)
    return value, second


def strain_kernel(table, applied, u, xm, ym, labels, top, second):
    row = lax.broadcasted_iota(jnp.int32, (32, 256), 0)
    inside = lax.broadcasted_iota(jnp.int32, (32, 256), 1) < 255

    def cells(x, here, there, r_here, r_there):
        d, s, dsh, ssh = [], [], [], []
        for c in range(3):
            d.append(there[c] - here[c])
            s.append(there[c] + here[c])
            dsh.append(jnp.where(row == 31, r_there[c] - r_here[c], pltpu.roll(d[c], 31, 0)))
            ssh.append(jnp.where(row == 31, r_there[c] + r_here[c], pltpu.roll(s[c], 31, 0)))
        plus, minus = combine(d, s, dsh, ssh)
        shifted = [pltpu.roll(p, 255, 1) for p in plus]
        value, second[x] = respond(
            applied,
            table,
            labels[x],
            [
                minus[0] + shifted[0],
                minus[1] + shifted[1],
                shifted[3] - minus[3],
                minus[2] + shifted[2],
                minus[4] + shifted[4],
                minus[5] + shifted[5],
            ],
        )
        top[x] = jnp.where(inside, value, 0.0)

    def step(x, carry):
        cells(
            x,
            [u[c, x] for c in range(3)],
            [u[c, x + 1] for c in range(3)],
            [ym[c, pl.ds(x, 1), :] for c in range(3)],
            [ym[c, pl.ds(x + 1, 1), :] for c in range(3)],
        )
        return carry

    lax.fori_loop(0, 31, step, 0)
    cells(
        31,
        [u[c, 31] for c in range(3)],
        [xm[c] for c in range(3)],
        [ym[c, 31:32, :] for c in range(3)],
        [ym[c, 32:33, :] for c in range(3)],
    )


def columns_out(field, out, first):
    def put(j, low, high):
        at = first + 16 * j
        out[at : at + 16, :] = jnp.concatenate([high, low], axis=0)

    edge_columns(
        lambda j, t: field[4 * j : 4 * j + 4, :, 128 * t : 128 * t + 128].reshape(128, 128), put
    )


def zpack_kernel(top, nodes, xm, ym, out):
    columns_out(top, out, 0)
    lane = lax.broadcasted_iota(jnp.int32, (32, 128), 1)
    lane1 = lax.broadcasted_iota(jnp.int32, (8, 128), 1)
    pad = jnp.zeros((88, 128), F32)
    for t in range(2):
        body = nodes[32 * t : 32 * t + 32, :]
        edge = jnp.zeros((8, 128), F32)
        for c in range(3):
            at = 40 * c + 32
            lanes = slice(128 * t, 128 * t + 128)
            body = jnp.where(lane == at, pltpu.roll(xm[c, :, lanes], (at + t) % 128, 1), body)
            turned = jnp.concatenate([ym[c, :, lanes], pad], axis=0).T
            line = turned[127:128] if t else turned[0:1]
            line = pltpu.roll(jnp.broadcast_to(line, (8, 128)), 40 * c, 1)
            edge = jnp.where((lane1 >= 40 * c) & (lane1 <= at), line, edge)
        out[128 + 40 * t : 160 + 40 * t, :] = body
        out[160 + 40 * t : 168 + 40 * t, :] = edge
    out[208:240, :] = nodes[64:96, :]


def column_cells(applied, table, lower, upper, lab):
    parts = []
    for n in (lower, upper):
        nx = pltpu.roll(n, 127, 1)
        d, s = nx - n, nx + n
        dsh, ssh = pltpu.roll(d, 39, 0), pltpu.roll(s, 39, 0)
        parts.append((d + dsh, ssh - s, ssh + s))
    gx = (parts[0][0] + parts[1][0])[0:32]
    gy = (parts[0][1] + parts[1][1])[0:32]
    gz = (parts[1][2] - parts[0][2])[0:32]
    gx = [gx, pltpu.roll(gx, 88, 1), pltpu.roll(gx, 48, 1)]
    gy = [gy, pltpu.roll(gy, 88, 1), pltpu.roll(gy, 48, 1)]
    gz = [gz, pltpu.roll(gz, 88, 1), pltpu.roll(gz, 48, 1)]
    return respond(
        applied,
        table,
        lab.astype(jnp.int32),
        [gx[0], gy[1], gz[2], gx[1] + gy[0], gy[2] + gz[1], gx[2] + gz[0]],
    )


def blocks_of(cells, scratch):
    keep = lax.broadcasted_iota(jnp.int32, (32, 128), 1) < 32
    padded = jnp.concatenate([jnp.where(keep, cells, 0.0), jnp.zeros((96, 128), F32)], axis=0)
    scratch[...] = padded.T[0:32]
    total = scratch[pl.ds(0, 8, stride=4), :]
    for i in range(1, 4):
        total = total + pltpu.roll(scratch[pl.ds(i, 8, stride=4), :], 32 * i, 1)
    return total


def z_local_kernel(field, gz, out):
    for j in range(8):
        hi, lo = split(field[4 * j : 4 * j + 4].reshape(128, 256))
        part = mxu(hi, gz[0], ((1,), (0,))) + mxu(lo, gz[0], ((1,), (0,)))
        part = part + mxu(hi, gz[1], ((1,), (0,)))
        out[4 * j : 4 * j + 4] = part.reshape(4, 32, 256)


def z_halo(local, halo, gh, out, before=None, last=None):
    for j in range(8):
        lines = halo[16 * j : 16 * j + 16, :]
        if before is None:
            rows = [lines, jnp.zeros((8, 128), F32)]
        else:
            rows = [lines[0:7], before[j : j + 1], lines[8:16], last[j : j + 1], jnp.zeros((7, 128), F32)]
        chi, clo = split(jnp.concatenate(rows, axis=0).T)
        c = jnp.concatenate([chi, clo, chi], axis=1)
        part = mxu(c, gh[...], ((1,), (0,))).reshape(4, 32, 256)
        out[4 * j : 4 * j + 4] = local[4 * j : 4 * j + 4] + part


def top_z_kernel(table, applied, odd, local, mine, peer, gh, out, near, far, second_last, scratch):
    last, second_last[...] = column_cells(
        applied, table, mine[168:208, :], peer[128:168, :], mine[208:240, :]
    )
    before, _ = column_cells(applied, table, peer[168:208, :], mine[128:168, :], peer[208:240, :])
    last, before = blocks_of(last, scratch), blocks_of(before, scratch)
    z_halo(local, peer, gh, out, before, last)
    y_edges(odd, out, near, far)


def weights_z_kernel(local, peer, gh, inverse):
    z_halo(local, peer, gh, inverse)
    inverse[...] = 1.0 / inverse[...]


def y_edges(odd, out, near, far):
    start = pl.multiple_of(24 * (1 - odd[1]), 8)
    near[...] = out[:, pl.ds(start, 8), :]
    far[...] = out[:, pl.ds(pl.multiple_of(24 - start, 8), 8), :]


def smooth_x(odd, cell, r_near, r_far, out):
    is_odd = odd[0] == 1
    table = taps()

    def step(k, carry):
        rows = pl.ds(pl.multiple_of((k // 2) * 8, 8), 8)
        lanes = pl.ds(pl.multiple_of((k % 2) * 128, 128), 128)
        low, high = [], []
        for i in range(8):
            a, b = r_near[i, rows, lanes], r_far[i, rows, lanes]
            low.append(jnp.where(is_odd, a, b))
            high.append(jnp.where(is_odd, b, a))
        cells = low + [cell(i, rows, lanes) for i in range(32)] + high
        for i in range(32):
            total = table[8] * cells[i + 8]
            for s in range(1, 9):
                total = total + table[8 + s] * (cells[i + 8 - s] + cells[i + 8 + s])
            out[i, rows, lanes] = total
        return carry

    lax.fori_loop(0, 8, step, 0)


def weights_x_kernel(table, odd, labels, r_near, r_far, out, near, far):
    smooth_x(odd, lambda *at: pick(labels[at], table, 2), r_near, r_far, out)
    y_edges(odd, out, near, far)


def smooth_y(x, is_odd, field, r_near, r_far, gy):
    a, b = r_near[x], r_far[x]
    cells = jnp.concatenate([jnp.where(is_odd, a, b), field[x], jnp.where(is_odd, b, a)], axis=0)
    hi, lo = split(cells)
    return mxu(gy[...], jnp.concatenate([hi, lo, hi], axis=0), ((1,), (0,)))


def smooth_all_y(odd, field, r_near, r_far, gy, out):
    is_odd = odd[1] == 1

    def step(x, carry):
        out[x] = smooth_y(x, is_odd, field, r_near, r_far, gy)
        return carry

    lax.fori_loop(0, 32, step, 0, unroll=8)


def weights_y_kernel(odd, field, r_near, r_far, gy, gz, out, cols):
    smooth_all_y(odd, field, r_near, r_far, gy, out)
    columns_out(out, cols, 0)
    z_local_kernel(out, gz, out)


def top_y_kernel(odd, field, r_near, r_far, gy, out, near, far):
    smooth_all_y(odd, field, r_near, r_far, gy, out)
    start = 24 * (1 - odd[0])
    near[...] = out[pl.ds(start, 8)]
    far[...] = out[pl.ds(24 - start, 8)]


def stress_kernel(table, labels, second, second_last, stress):
    lane = lax.broadcasted_iota(jnp.int32, (32, 128), 1)

    def step(x, carry):
        moved = pltpu.roll(second_last[...], 127 - x, 1)
        end = jnp.where(lane == 127, moved, second[x, :, 128:256])
        whole = jnp.concatenate([second[x, :, 0:128], end], axis=1)
        stress[x] = pick(labels[x], table, 3) * jnp.sqrt(whole)
        return carry

    lax.fori_loop(0, 32, step, 0, unroll=2)


def finish_cells(table, lab, averaged, history, stress):
    kappa = jnp.maximum(history, averaged)
    start = pick(lab, table, 4)
    grown = (
        1.0
        - pick(lab, table, 5) / jnp.maximum(kappa, start)
        - pick(lab, table, 6) * jnp.exp(pick(lab, table, 7) * (start - kappa))
    )
    harm = jnp.where(kappa > start, grown, 0.0)
    return harm, (1.0 - harm) * stress


def finish_planes(
    table, window, count, first, inverse, history, stress, labels, d_buf, m_buf, damage, mises, sem
):
    g = taps()

    def step(k):
        rows = pl.ds(pl.multiple_of((k // 2) * 8, 8), 8)
        lanes = pl.ds(pl.multiple_of((k % 2) * 128, 128), 128)
        cells = [window(w, rows, lanes) for w in range(count + 16)]
        for i in range(count):
            total = g[8] * cells[i + 8]
            for s in range(1, 9):
                total = total + g[8 + s] * (cells[i + 8 - s] + cells[i + 8 + s])
            at = (first + i, rows, lanes)
            harm, von_mises = finish_cells(
                table, labels[at], total * inverse[at], history[at], stress[at]
            )
            d_buf[i, rows, lanes] = harm
            m_buf[i, rows, lanes] = von_mises

    def copies(t):
        rows = slice(8 * t, 8 * t + 8)
        place = (pl.ds(first, count), rows)
        return [
            pltpu.make_async_copy(d_buf.at[:, rows], damage.at[place], sem.at[0, t]),
            pltpu.make_async_copy(m_buf.at[:, rows], mises.at[place], sem.at[1, t]),
        ]

    for t in range(4):

        def half(k, carry, t=t):
            step(2 * t + k)
            return carry

        lax.fori_loop(0, 2, half, 0)
        for copy in copies(t):
            copy.start()
    for t in range(4):
        for copy in copies(t):
            copy.wait()


def finish_most_kernel(
    table, odd, field, near, inverse, history, stress, labels, damage, mises, d_buf, m_buf, sem
):
    is_odd, shift = odd[0] == 1, 8 * odd[0]

    def window(w, rows, lanes):
        if w < 8:
            return jnp.where(is_odd, near[w, rows, lanes], field[w, rows, lanes])
        if w < 32:
            return field[w - shift, rows, lanes]
        return jnp.where(is_odd, field[w - 8, rows, lanes], near[w - 32, rows, lanes])

    first = 8 - shift
    finish_planes(
        table, window, 24, first, inverse, history, stress, labels, d_buf, m_buf, damage, mises, sem
    )


def finish_rest_kernel(
    table, odd, field, far, inverse, history, stress, labels, d_in, m_in, damage, mises, d_buf, m_buf, sem
):
    del d_in, m_in
    is_odd, shift = odd[0] == 1, 8 * odd[0]

    def window(w, rows, lanes):
        if w < 8:
            return jnp.where(is_odd, field[16 + w, rows, lanes], far[w, rows, lanes])
        if w < 16:
            return field[w - 8 + 3 * shift, rows, lanes]
        return jnp.where(is_odd, far[w - 16, rows, lanes], field[w - 8, rows, lanes])

    first = 3 * shift
    finish_planes(
        table, window, 8, first, inverse, history, stress, labels, d_buf, m_buf, damage, mises, sem
    )


def shards(
    displacement,
    applied_strain,
    labels,
    history,
    modulus,
    poisson,
    threshold,
    ductility,
    brittleness,
    weight,
):
    (table,) = call(
        table_kernel, [(8, 4)], n_in=6, smem=range(6), out_spaces=[pltpu.SMEM], limit=1 << 20
    )(modulus, poisson, threshold, ductility, brittleness, weight)
    gz = jnp.stack([jnp.asarray(m) for m in split_const(band(256, 256, 0).T)])
    low, high = band(256, 8, -8).T, band(256, 8, 256).T
    own = band(256, 256, 0).T[255:256]
    h_hi, h_lo = split_const(np.concatenate([low, high, own, np.zeros((7, 256))], axis=0))
    gh = jnp.asarray(np.concatenate([h_hi, h_hi, h_lo], axis=0))
    y_hi, y_lo = split_const(band(32, 48, -8))
    gy = jnp.asarray(np.concatenate([y_hi, y_hi, y_lo], axis=1))

    field3, edge_x, edge_y = (32, 32, 256), (8, 32, 256), (32, 8, 256)
    hbm, vmem, dma = pltpu.HBM, pltpu.VMEM, pltpu.SemaphoreType.DMA
    xm, ym, displacement = call(
        planes_kernel, [(3, 32, 256), (3, 32, 256), displacement.shape], scratch=[dma((1,))]
    )(displacement)
    x_token = xm
    xm = shift_route(xm, ("gx",), (-1,))
    near, far = call(
        weight_edges_kernel, [edge_x, edge_x], spaces=[None, hbm],
        scratch=[vmem(edge_x, jnp.int32), vmem(edge_x, jnp.int32), dma((2,))], smem=(0,), odd=1,
        after=(x_token,),
    )(weight, labels)
    w_near, w_far = swap_route(near, "gx", 0), swap_route(far, "gx", 1)
    (ym,) = call(extend_kernel, [(3, 40, 256)], n_in=2, after=(near,))(ym, xm)
    y_token = ym
    ym = shift_route(ym, ("gy",), (-1,))
    (nodes,) = call(columns_kernel, [(96, 128)], n_in=2, after=(y_token,))(displacement, labels)
    top, second = call(strain_kernel, [field3, field3], n_in=6, smem=(0, 1))(
        table, applied_strain, displacement, xm, ym, labels
    )
    (mine,) = call(zpack_kernel, [(240, 128)], n_in=4)(top, nodes, xm, ym)
    peer = shift_route(mine, ("gz",), (1,))
    weights, near, far = call(
        weights_x_kernel, [field3, edge_y, edge_y], n_in=4, smem=(0,), odd=1, after=(mine,)
    )(table, labels, w_near, w_far)
    w_near, w_far = swap_route(near, "gy", 0), swap_route(far, "gy", 1)
    (local,) = call(z_local_kernel, [field3], n_in=2, after=(near,))(top, gz)
    top, near, far, second_last = call(
        top_z_kernel, [field3, edge_y, edge_y, (32, 128)], scratch=[vmem((32, 128), F32)], n_in=6, smem=(0, 1), odd=2
    )(table, applied_strain, local, mine, peer, gh)
    t_near, t_far = swap_route(near, "gy", 0), swap_route(far, "gy", 1)
    weights, cols = call(
        weights_y_kernel, [field3, (128, 128)], n_in=5, odd=0, after=(near,)
    )(weights, w_near, w_far, gy, gz)
    z_token = cols
    cols = shift_route(cols, ("gz",), (1,))
    (stress,) = call(stress_kernel, [field3], n_in=4, smem=(0,), after=(z_token,))(table, labels, second, second_last)
    top, near, far = call(top_y_kernel, [field3, edge_x, edge_x], n_in=4, odd=0, after=(stress,))(
        top, t_near, t_far, gy
    )
    (inverse,) = call(weights_z_kernel, [field3], n_in=3, after=(near,))(weights, cols, gh)
    near, far = swap_route(near, "gx", 0), swap_route(far, "gx", 1)
    outs = [field3, field3]
    damage, mises = call(
        finish_most_kernel, outs, n_in=7, smem=(0,), odd=1, out_spaces=[hbm, hbm],
        scratch=[vmem((24, 32, 256), F32), vmem((24, 32, 256), F32), dma((2, 4))],
    )(table, top, near, inverse, history, stress, labels)
    return call(
        finish_rest_kernel, outs, smem=(0,), odd=1, out_spaces=[hbm, hbm],
        spaces=[None] * 7 + [hbm, hbm], aliases={7: 0, 8: 1},
        scratch=[vmem((8, 32, 256), F32), vmem((8, 32, 256), F32), dma((2, 4))],
    )(table, top, far, inverse, history, stress, labels, damage, mises)


def solution(mesh):
    cells = P("gx", "gy", "gz")
    placed = (P(None, "gx", "gy", "gz"), P(), cells, cells, P(), P(), P(), P(), P(), P())

    def body(*args):
        return tuple(shards(*args))

    return jax.shard_map(
        body, mesh=mesh, in_specs=placed, out_specs=(cells, cells), check_vma=False
    )
```

```python
import math

import jax
import jax.numpy as jnp
import numpy as np
from jax import lax
from jax.experimental import pallas as pl
from jax.experimental.pallas import tpu as pltpu
from jax.sharding import PartitionSpec as P


RADIUS = 8
F32 = jnp.float32
BF16 = jnp.bfloat16


def taps():
    return [math.exp(-2.0 * s * s / (RADIUS * RADIUS)) for s in range(-RADIUS, RADIUS + 1)]


def band(outs, ins, offset):
    table = taps()
    full = np.zeros((outs, ins), np.float64)
    for i in range(outs):
        for k in range(ins):
            s = k + offset - i
            if abs(s) <= RADIUS:
                full[i, k] = table[s + RADIUS]
    return full


def split_const(full):
    hi = full.astype(jnp.bfloat16)
    lo = (full - hi.astype(np.float64)).astype(jnp.bfloat16)
    return hi, lo


def split(f):
    hi = f.astype(BF16)
    lo = (f - hi.astype(F32)).astype(BF16)
    return hi, lo


def mxu(a, b, dims):
    return lax.dot_general(a, b, (dims, ((), ())), preferred_element_type=F32)


def shift_route(block, axes, steps):
    sizes = [lax.axis_size(a) for a in axes]
    total = math.prod(sizes)
    route = []
    for flat in range(total):
        place = np.unravel_index(flat, sizes)
        target = tuple((i + s) % n for i, s, n in zip(place, steps, sizes))
        route.append((flat, int(np.ravel_multi_index(target, sizes))))
    return lax.ppermute(block, axes if len(axes) > 1 else axes[0], route)


def swap_route(block, axis, parity):
    size = lax.axis_size(axis)
    route = []
    for k in range(0, size, 2):
        a, b = (k + parity) % size, (k + 1 + parity) % size
        route += [(a, b), (b, a)]
    return lax.ppermute(block, axis, route)


def call(
    kernel, outs, scratch=(), n_in=1, smem=(), limit=10 << 20, spaces=None, out_spaces=None,
    aliases=None, after=(), odd=None,
):
    spaces = (spaces or [None] * n_in) + [pl.ANY] * len(after)
    n_in = len(spaces) - len(after)

    def body(*refs):
        refs = [*refs[:n_in], *refs[n_in + len(after) :]]
        if odd is not None:
            refs.insert(odd, (lax.axis_index("gx") % 2, lax.axis_index("gy") % 2))
        kernel(*refs)

    specs = [
        pl.BlockSpec(memory_space=pltpu.SMEM if i in smem else space or pltpu.VMEM)
        for i, space in enumerate(spaces)
    ]
    built = pl.pallas_call(
        body,
        out_shape=[jax.ShapeDtypeStruct(s, F32) for s in outs],
        in_specs=specs,
        out_specs=[pl.BlockSpec(memory_space=s) for s in out_spaces or [pltpu.VMEM] * len(outs)],
        scratch_shapes=list(scratch),
        input_output_aliases=aliases or {},
        compiler_params=pltpu.CompilerParams(vmem_limit_bytes=limit),
    )
    return lambda *args: built(*args, *after)


def pick(labels, entries):
    out = jnp.where(labels == 0, entries[0], entries[3])
    out = jnp.where(labels == 1, entries[1], out)
    return jnp.where(labels == 2, entries[2], out)


def each(fn, *params):
    return [fn(*(p[k] for p in params)) for k in range(4)]


def edge_columns(field, put):
    for j in range(8):
        put(j, field(j, 0).T[0:8], field(j, 1).T[120:128])


def planes_kernel(u, xm, ym, xym, kept, sem):
    keep = pltpu.make_async_copy(u, kept, sem.at[0])
    keep.start()
    for c in range(3):
        xm[c] = u[c, 0]
        for x in range(32):
            ym[c, x : x + 1, :] = u[c, x, 0:1, :]
        xym[c : c + 1, :] = u[c, 0, 0:1, :]
    keep.wait()


def weight_edges_kernel(weight, odd, labels, near, far, low, high, sem):
    copies = [
        pltpu.make_async_copy(labels.at[pl.ds(0, 8)], low, sem.at[0]),
        pltpu.make_async_copy(labels.at[pl.ds(24, 8)], high, sem.at[1]),
    ]
    for copy in copies:
        copy.start()
    for copy in copies:
        copy.wait()
    is_odd = odd[0] == 1

    def step(i, carry):
        a, b = pick(low[i], weight), pick(high[i], weight)
        near[i] = jnp.where(is_odd, a, b)
        far[i] = jnp.where(is_odd, b, a)
        return carry

    lax.fori_loop(0, 8, step, 0, unroll=2)


def columns_kernel(u, labels, nodes):
    lane = lax.broadcasted_iota(jnp.int32, (32, 128), 1)

    def step(x, carry):
        first, last, lab = carry
        for c in range(3):
            at = 40 * c + x
            first = jnp.where(lane == at, pltpu.roll(u[c, x, :, 0:128], at, 1), first)
            last = jnp.where(lane == at, pltpu.roll(u[c, x, :, 128:256], at + 1, 1), last)
        moved = pltpu.roll(labels[x, :, 128:256], x + 1, 1)
        return first, last, jnp.where(lane == x, moved, lab)

    zero = jnp.zeros((32, 128), F32)
    first, last, lab = lax.fori_loop(
        0, 32, step, (zero, zero, jnp.zeros((32, 128), jnp.int32)), unroll=8
    )
    nodes[0:32, :] = first
    nodes[32:64, :] = last
    nodes[64:96, :] = lab.astype(F32)


def combine(d, s, dsh, ssh):
    a = [d[c] + dsh[c] for c in range(3)]
    b = [ssh[c] - s[c] for c in range(3)]
    m = [ssh[c] + s[c] for c in range(3)]
    plus = [a[0], b[1], a[1] + b[0], m[2], b[2] + m[1], a[2] + m[0]]
    minus = [a[0], b[1], a[1] + b[0], m[2], b[2] - m[1], a[2] - m[0]]
    return plus, minus


def root(t):
    return t * lax.rsqrt(jnp.maximum(t, 1e-37))


def response(poisson, weight):
    lead = each(lambda nu, w: 0.1125 * w / (1.0 - 2.0 * nu), poisson, weight)
    shear = each(lambda nu, w: w / (1.0 + nu), poisson, weight)
    return lead, [(0.3 / 96.0) * (f * f) for f in shear]


def respond(applied, law, lab, sums):
    xx, yy, zz = (4.0 * applied[i] + sums[i] for i in range(3))
    xy, yz, xz = (8.0 * applied[i] + sums[j] for i, j in ((5, 3), (3, 4), (4, 5)))
    trace = xx + yy + zz
    p, q, r = xx - yy, yy - zz, zz - xx
    second = (p * p + q * q + r * r) + 1.5 * (yz * yz + xz * xz + xy * xy)
    lead = pick(lab, law[0]) * trace
    return lead + root(lead * lead + pick(lab, law[1]) * second), second


def strain_kernel(weight, poisson, applied, u, xm, ym, xym, labels, top, second):
    end = lax.broadcasted_iota(jnp.int32, (8, 256), 0) == 7
    inside = lax.broadcasted_iota(jnp.int32, (8, 128), 1) < 127
    law = response(poisson, weight)

    def cells(x, here, there, r_here, r_there):
        below = [
            jnp.broadcast_to(line, (8, 256))
            for c in range(3)
            for line in (r_there[c] - r_here[c], r_there[c] + r_here[c])
        ]
        for k in (3, 2, 1, 0):
            rows = slice(8 * k, 8 * k + 8)
            d, s, dsh, ssh, turned = [], [], [], [], []
            for c in range(3):
                a, b = here(c, rows), there(c, rows)
                d.append(b - a)
                s.append(b + a)
                turned += [pltpu.roll(d[c], 7, 0), pltpu.roll(s[c], 7, 0)]
                dsh.append(jnp.where(end, below[2 * c], turned[2 * c]))
                ssh.append(jnp.where(end, below[2 * c + 1], turned[2 * c + 1]))
            below = turned
            plus, minus = combine(d, s, dsh, ssh)
            shifted = [pltpu.roll(p, 255, 1) for p in plus]
            value, second[x, rows, :] = respond(
                applied,
                law,
                labels[x, rows, :],
                [
                    minus[0] + shifted[0],
                    minus[1] + shifted[1],
                    shifted[3] - minus[3],
                    minus[2] + shifted[2],
                    minus[4] + shifted[4],
                    minus[5] + shifted[5],
                ],
            )
            top[x, rows, 0:128] = value[:, 0:128]
            top[x, rows, 128:256] = jnp.where(inside, value[:, 128:256], 0.0)

    def step(x, carry):
        cells(
            x,
            lambda c, rows: u[c, x, rows, :],
            lambda c, rows: u[c, x + 1, rows, :],
            [ym[c, pl.ds(x, 1), :] for c in range(3)],
            [ym[c, pl.ds(x + 1, 1), :] for c in range(3)],
        )
        return carry

    lax.fori_loop(0, 31, step, 0)
    cells(
        31,
        lambda c, rows: u[c, 31, rows, :],
        lambda c, rows: xm[c, rows, :],
        [ym[c, 31:32, :] for c in range(3)],
        [xym[c : c + 1, :] for c in range(3)],
    )


def columns_out(field, out, first):
    def put(j, low, high):
        at = first + 16 * j
        out[at : at + 16, :] = jnp.concatenate([high, low], axis=0)

    edge_columns(
        lambda j, t: field[4 * j : 4 * j + 4, :, 128 * t : 128 * t + 128].reshape(128, 128), put
    )


def zpack_kernel(top, nodes, xm, ym, xym, out):
    columns_out(top, out, 0)
    lane = lax.broadcasted_iota(jnp.int32, (32, 128), 1)
    lane1 = lax.broadcasted_iota(jnp.int32, (8, 128), 1)
    pad = jnp.zeros((96, 128), F32)
    for t in range(2):
        body = nodes[32 * t : 32 * t + 32, :]
        edge = jnp.zeros((8, 128), F32)
        for c in range(3):
            at = 40 * c + 32
            lanes = slice(128 * t, 128 * t + 128)
            body = jnp.where(lane == at, pltpu.roll(xm[c, :, lanes], (at + t) % 128, 1), body)
            turned = jnp.concatenate([ym[c, :, lanes], pad], axis=0).T
            line = turned[127:128] if t else turned[0:1]
            line = pltpu.roll(jnp.broadcast_to(line, (8, 128)), 40 * c, 1)
            corner = pltpu.roll(jnp.broadcast_to(xym[c : c + 1, lanes], (8, 128)), (at + t) % 128, 1)
            edge = jnp.where((lane1 >= 40 * c) & (lane1 < at), line, edge)
            edge = jnp.where(lane1 == at, corner, edge)
        out[128 + 40 * t : 160 + 40 * t, :] = body
        out[160 + 40 * t : 168 + 40 * t, :] = edge
    out[208:240, :] = nodes[64:96, :]


def column_cells(applied, law, lower, upper, lab):
    parts = []
    for n in (lower, upper):
        nx = pltpu.roll(n, 127, 1)
        d, s = nx - n, nx + n
        dsh, ssh = pltpu.roll(d, 39, 0), pltpu.roll(s, 39, 0)
        parts.append((d + dsh, ssh - s, ssh + s))
    gx = (parts[0][0] + parts[1][0])[0:32]
    gy = (parts[0][1] + parts[1][1])[0:32]
    gz = (parts[1][2] - parts[0][2])[0:32]
    gx = [gx, pltpu.roll(gx, 88, 1), pltpu.roll(gx, 48, 1)]
    gy = [gy, pltpu.roll(gy, 88, 1), pltpu.roll(gy, 48, 1)]
    gz = [gz, pltpu.roll(gz, 88, 1), pltpu.roll(gz, 48, 1)]
    return respond(
        applied,
        law,
        lab.astype(jnp.int32),
        [gx[0], gy[1], gz[2], gx[1] + gy[0], gy[2] + gz[1], gx[2] + gz[0]],
    )


def blocks_of(cells, scratch):
    keep = lax.broadcasted_iota(jnp.int32, (32, 128), 1) < 32
    padded = jnp.concatenate([jnp.where(keep, cells, 0.0), jnp.zeros((96, 128), F32)], axis=0)
    scratch[...] = padded.T[0:32]
    total = scratch[pl.ds(0, 8, stride=4), :]
    for i in range(1, 4):
        total = total + pltpu.roll(scratch[pl.ds(i, 8, stride=4), :], 32 * i, 1)
    return total


def z_local_kernel(field, gz, out):
    for j in range(8):
        hi, lo = split(field[4 * j : 4 * j + 4].reshape(128, 256))
        part = mxu(hi, gz[0], ((1,), (0,))) + mxu(lo, gz[0], ((1,), (0,)))
        part = part + mxu(hi, gz[1], ((1,), (0,)))
        out[4 * j : 4 * j + 4] = part.reshape(4, 32, 256)


def z_halo(local, halo, gh, out, before=None, last=None):
    for j in range(8):
        lines = halo[16 * j : 16 * j + 16, :]
        if before is None:
            rows = [lines, jnp.zeros((8, 128), F32)]
        else:
            rows = [lines[0:7], before[j : j + 1], lines[8:16], last[j : j + 1], jnp.zeros((7, 128), F32)]
        chi, clo = split(jnp.concatenate(rows, axis=0).T)
        c = jnp.concatenate([chi, clo, chi], axis=1)
        part = mxu(c, gh[...], ((1,), (0,))).reshape(4, 32, 256)
        out[4 * j : 4 * j + 4] = local[4 * j : 4 * j + 4] + part


def top_z_kernel(weight, poisson, applied, odd, local, mine, peer, gh, out, near, far, second_last, scratch):
    law = response(poisson, weight)
    last, second_last[...] = column_cells(
        applied, law, mine[168:208, :], peer[128:168, :], mine[208:240, :]
    )
    before, _ = column_cells(applied, law, peer[168:208, :], mine[128:168, :], peer[208:240, :])
    last, before = blocks_of(last, scratch), blocks_of(before, scratch)
    z_halo(local, peer, gh, out, before, last)
    y_edges(odd, out, near, far)


def weights_z_kernel(local, peer, gh, inverse):
    z_halo(local, peer, gh, inverse)
    inverse[...] = 1.0 / inverse[...]


def y_edges(odd, out, near, far):
    start = pl.multiple_of(24 * (1 - odd[1]), 8)
    near[...] = out[:, pl.ds(start, 8), :]
    far[...] = out[:, pl.ds(pl.multiple_of(24 - start, 8), 8), :]


def smooth_x(odd, cell, r_near, r_far, out):
    is_odd = odd[0] == 1
    table = taps()

    def step(k, carry):
        rows = pl.ds(pl.multiple_of((k // 2) * 8, 8), 8)
        lanes = pl.ds(pl.multiple_of((k % 2) * 128, 128), 128)
        low, high = [], []
        for i in range(8):
            a, b = r_near[i, rows, lanes], r_far[i, rows, lanes]
            low.append(jnp.where(is_odd, a, b))
            high.append(jnp.where(is_odd, b, a))
        cells = low + [cell(i, rows, lanes) for i in range(32)] + high
        for i in range(32):
            total = table[8] * cells[i + 8]
            for s in range(1, 9):
                total = total + table[8 + s] * (cells[i + 8 - s] + cells[i + 8 + s])
            out[i, rows, lanes] = total
        return carry

    lax.fori_loop(0, 8, step, 0)


def weights_x_kernel(weight, odd, labels, r_near, r_far, out, near, far):
    smooth_x(odd, lambda *at: pick(labels[at], weight), r_near, r_far, out)
    y_edges(odd, out, near, far)


def smooth_y(x, is_odd, field, r_near, r_far, gy):
    a, b = r_near[x], r_far[x]
    cells = jnp.concatenate([jnp.where(is_odd, a, b), field[x], jnp.where(is_odd, b, a)], axis=0)
    hi, lo = split(cells)
    return mxu(gy[...], jnp.concatenate([hi, lo, hi], axis=0), ((1,), (0,)))


def smooth_all_y(odd, field, r_near, r_far, gy, out):
    is_odd = odd[1] == 1

    def step(x, carry):
        out[x] = smooth_y(x, is_odd, field, r_near, r_far, gy)
        return carry

    lax.fori_loop(0, 32, step, 0, unroll=8)


def weights_y_kernel(odd, field, r_near, r_far, gy, gz, out, cols):
    smooth_all_y(odd, field, r_near, r_far, gy, out)
    columns_out(out, cols, 0)
    z_local_kernel(out, gz, out)


def top_y_kernel(odd, field, r_near, r_far, gy, out, near, far):
    smooth_all_y(odd, field, r_near, r_far, gy, out)
    start = 24 * (1 - odd[0])
    near[...] = out[pl.ds(start, 8)]
    far[...] = out[pl.ds(24 - start, 8)]


def phases_kernel(
    modulus, poisson, threshold, ductility, brittleness,
    labels, second, second_last, stress, start, lost, ductile, brittle,
):
    lane = lax.broadcasted_iota(jnp.int32, (32, 128), 1)
    stiff = each(lambda e, nu: math.sqrt(3.0 / 96.0) * e / (1.0 + nu), modulus, poisson)
    gone = each(lambda k, a: k * (1.0 - a), threshold, ductility)
    rate = each(lambda b: b * math.log2(math.e), brittleness)

    def step(x, carry):
        lab = labels[x]
        moved = pltpu.roll(second_last[...], 127 - x, 1)
        end = jnp.where(lane == 127, moved, second[x, :, 128:256])
        whole = jnp.concatenate([second[x, :, 0:128], end], axis=1)
        stress[x] = pick(lab, stiff) * root(whole)
        start[x] = pick(lab, threshold)
        lost[x] = pick(lab, gone)
        ductile[x] = pick(lab, ductility)
        brittle[x] = pick(lab, rate)
        return carry

    lax.fori_loop(0, 32, step, 0, unroll=4)


def finish_cells(averaged, history, stress, start, lost, ductile, brittle):
    kappa = jnp.maximum(history, averaged)
    grown = 1.0 - lost / kappa - ductile * jnp.exp2(brittle * (start - kappa))
    harm = jnp.where(kappa > start, grown, 0.0)
    return harm, (1.0 - harm) * stress


def finish_planes(window, count, first, inverse, fields, d_buf, m_buf, damage, mises, sem):
    g = taps()

    def step(k):
        rows = pl.ds(pl.multiple_of((k // 2) * 8, 8), 8)
        lanes = pl.ds(pl.multiple_of((k % 2) * 128, 128), 128)
        cells = [window(w, rows, lanes) for w in range(count + 16)]
        for i in range(count):
            total = g[8] * cells[i + 8]
            for s in range(1, 9):
                total = total + g[8 + s] * (cells[i + 8 - s] + cells[i + 8 + s])
            at = (first + i, rows, lanes)
            harm, von_mises = finish_cells(total * inverse[at], *(f[at] for f in fields))
            d_buf[i, rows, lanes] = harm
            m_buf[i, rows, lanes] = von_mises

    def copies(t):
        rows = slice(8 * t, 8 * t + 8)
        place = (pl.ds(first, count), rows)
        return [
            pltpu.make_async_copy(d_buf.at[:, rows], damage.at[place], sem.at[0, t]),
            pltpu.make_async_copy(m_buf.at[:, rows], mises.at[place], sem.at[1, t]),
        ]

    for t in range(4):

        def half(k, carry, t=t):
            step(2 * t + k)
            return carry

        lax.fori_loop(0, 2, half, 0)
        for copy in copies(t):
            copy.start()
    for t in range(4):
        for copy in copies(t):
            copy.wait()


def finish_most_kernel(odd, field, near, inverse, *refs):
    is_odd, shift = odd[0] == 1, 8 * odd[0]

    def window(w, rows, lanes):
        if w < 8:
            return jnp.where(is_odd, near[w, rows, lanes], field[w, rows, lanes])
        if w < 32:
            return field[w - shift, rows, lanes]
        return jnp.where(is_odd, field[w - 8, rows, lanes], near[w - 32, rows, lanes])

    first = 8 - shift
    damage, mises, d_buf, m_buf, sem = refs[6:]
    finish_planes(window, 24, first, inverse, refs[:6], d_buf, m_buf, damage, mises, sem)


def finish_rest_kernel(odd, field, far, inverse, *refs):
    is_odd, shift = odd[0] == 1, 8 * odd[0]

    def window(w, rows, lanes):
        if w < 8:
            return jnp.where(is_odd, field[16 + w, rows, lanes], far[w, rows, lanes])
        if w < 16:
            return field[w - 8 + 3 * shift, rows, lanes]
        return jnp.where(is_odd, far[w - 16, rows, lanes], field[w - 8, rows, lanes])

    first = 3 * shift
    damage, mises, d_buf, m_buf, sem = refs[8:]
    finish_planes(window, 8, first, inverse, refs[:6], d_buf, m_buf, damage, mises, sem)


def shards(
    displacement,
    applied_strain,
    labels,
    history,
    modulus,
    poisson,
    threshold,
    ductility,
    brittleness,
    weight,
):
    gz = jnp.stack([jnp.asarray(m) for m in split_const(band(256, 256, 0).T)])
    low, high = band(256, 8, -8).T, band(256, 8, 256).T
    own = band(256, 256, 0).T[255:256]
    h_hi, h_lo = split_const(np.concatenate([low, high, own, np.zeros((7, 256))], axis=0))
    gh = jnp.asarray(np.concatenate([h_hi, h_hi, h_lo], axis=0))
    y_hi, y_lo = split_const(band(32, 48, -8))
    gy = jnp.asarray(np.concatenate([y_hi, y_hi, y_lo], axis=1))

    field3, edge_x, edge_y = (32, 32, 256), (8, 32, 256), (32, 8, 256)
    hbm, vmem, dma = pltpu.HBM, pltpu.VMEM, pltpu.SemaphoreType.DMA
    xm, ym, xym, displacement = call(
        planes_kernel, [(3, 32, 256), (3, 32, 256), (8, 256), displacement.shape], scratch=[dma((1,))],
    )(displacement)
    x_token = xm
    xm = shift_route(xm, ("gx",), (-1,))
    ym = shift_route(ym, ("gy",), (-1,))
    xym = shift_route(xym, ("gx", "gy"), (-1, -1))
    near, far = call(
        weight_edges_kernel, [edge_x, edge_x], spaces=[None, hbm],
        scratch=[vmem(edge_x, jnp.int32), vmem(edge_x, jnp.int32), dma((2,))], smem=(0,), odd=1,
        after=(x_token,),
    )(weight, labels)
    w_near = swap_route(near, "gx", 0)
    w_far = swap_route(far, "gx", 1)
    (nodes,) = call(columns_kernel, [(96, 128)], n_in=2, after=(near,))(displacement, labels)
    top, second = call(strain_kernel, [field3, field3], n_in=8, smem=(0, 1, 2))(
        weight, poisson, applied_strain, displacement, xm, ym, xym, labels
    )
    (mine,) = call(zpack_kernel, [(240, 128)], n_in=5)(top, nodes, xm, ym, xym)
    peer = shift_route(mine, ("gz",), (1,))
    weights, near, far = call(
        weights_x_kernel, [field3, edge_y, edge_y], n_in=4, smem=(0,), odd=1, after=(mine,)
    )(weight, labels, w_near, w_far)
    w_near, w_far = swap_route(near, "gy", 0), swap_route(far, "gy", 1)
    (local,) = call(z_local_kernel, [field3], n_in=2, after=(near,))(top, gz)
    top, near, far, second_last = call(
        top_z_kernel, [field3, edge_y, edge_y, (32, 128)], scratch=[vmem((32, 128), F32)], n_in=7, smem=(0, 1, 2), odd=3
    )(weight, poisson, applied_strain, local, mine, peer, gh)
    t_near, t_far = swap_route(near, "gy", 0), swap_route(far, "gy", 1)
    phases = call(
        phases_kernel, [field3] * 5, n_in=8, smem=range(5), after=(near,)
    )(modulus, poisson, threshold, ductility, brittleness, labels, second, second_last)
    weights, cols = call(
        weights_y_kernel, [field3, (128, 128)], n_in=5, odd=0, after=(phases[0],)
    )(weights, w_near, w_far, gy, gz)
    z_token = cols
    cols = shift_route(cols, ("gz",), (1,))
    top, near, far = call(
        top_y_kernel, [field3, edge_x, edge_x], n_in=4, odd=0, after=(z_token,)
    )(top, t_near, t_far, gy)
    (inverse,) = call(weights_z_kernel, [field3], n_in=3, after=(near,))(weights, cols, gh)
    far = swap_route(far, "gx", 1)
    near = swap_route(near, "gx", 0)
    outs = [field3, field3]
    fields = (inverse, history, *phases)
    damage, mises = call(
        finish_most_kernel, outs, n_in=9, odd=0, out_spaces=[hbm, hbm],
        scratch=[vmem((24, 32, 256), F32), vmem((24, 32, 256), F32), dma((2, 4))],
    )(top, near, *fields)
    return call(
        finish_rest_kernel, outs, odd=0, out_spaces=[hbm, hbm],
        spaces=[None] * 9 + [hbm, hbm], aliases={9: 0, 10: 1},
        scratch=[vmem((8, 32, 256), F32), vmem((8, 32, 256), F32), dma((2, 4))],
    )(top, far, *fields, damage, mises)


def solution(mesh):
    cells = P("gx", "gy", "gz")
    placed = (P(None, "gx", "gy", "gz"), P(), cells, cells, P(), P(), P(), P(), P(), P())

    def body(*args):
        return tuple(shards(*args))

    return jax.shard_map(
        body, mesh=mesh, in_specs=placed, out_specs=(cells, cells), check_vma=False
    )
```

```python
import math

import jax
import jax.numpy as jnp
import numpy as np
from jax import lax
from jax.experimental import pallas as pl
from jax.experimental.pallas import tpu as pltpu
from jax.sharding import PartitionSpec as P


RADIUS = 8
F32 = jnp.float32
BF16 = jnp.bfloat16


def taps():
    return [math.exp(-2.0 * s * s / (RADIUS * RADIUS)) for s in range(-RADIUS, RADIUS + 1)]


def band(outs, ins, offset):
    table = taps()
    full = np.zeros((outs, ins), np.float64)
    for i in range(outs):
        for k in range(ins):
            s = k + offset - i
            if abs(s) <= RADIUS:
                full[i, k] = table[s + RADIUS]
    return full


def split_const(full):
    hi = full.astype(jnp.bfloat16)
    lo = (full - hi.astype(np.float64)).astype(jnp.bfloat16)
    return hi, lo


def split(f):
    hi = f.astype(BF16)
    lo = (f - hi.astype(F32)).astype(BF16)
    return hi, lo


def mxu(a, b, dims):
    return lax.dot_general(a, b, (dims, ((), ())), preferred_element_type=F32)


def shift_route(block, axes, steps):
    sizes = [lax.axis_size(a) for a in axes]
    total = math.prod(sizes)
    route = []
    for flat in range(total):
        place = np.unravel_index(flat, sizes)
        target = tuple((i + s) % n for i, s, n in zip(place, steps, sizes))
        route.append((flat, int(np.ravel_multi_index(target, sizes))))
    return lax.ppermute(block, axes if len(axes) > 1 else axes[0], route)


def swap_route(block, axis, parity):
    size = lax.axis_size(axis)
    route = []
    for k in range(0, size, 2):
        a, b = (k + parity) % size, (k + 1 + parity) % size
        route += [(a, b), (b, a)]
    return lax.ppermute(block, axis, route)


def call(
    kernel, outs, scratch=(), n_in=1, smem=(), limit=10 << 20, spaces=None, out_spaces=None,
    aliases=None, after=(), odd=None,
):
    spaces = (spaces or [None] * n_in) + [pl.ANY] * len(after)
    n_in = len(spaces) - len(after)

    def body(*refs):
        refs = [*refs[:n_in], *refs[n_in + len(after) :]]
        if odd is not None:
            refs.insert(odd, (lax.axis_index("gx") % 2, lax.axis_index("gy") % 2))
        kernel(*refs)

    specs = [
        pl.BlockSpec(memory_space=pltpu.SMEM if i in smem else space or pltpu.VMEM)
        for i, space in enumerate(spaces)
    ]
    built = pl.pallas_call(
        body,
        out_shape=[jax.ShapeDtypeStruct(s, F32) for s in outs],
        in_specs=specs,
        out_specs=[pl.BlockSpec(memory_space=s) for s in out_spaces or [pltpu.VMEM] * len(outs)],
        scratch_shapes=list(scratch),
        input_output_aliases=aliases or {},
        compiler_params=pltpu.CompilerParams(vmem_limit_bytes=limit),
    )
    return lambda *args: built(*args, *after)


def pick(labels, entries):
    out = jnp.where(labels == 0, entries[0], entries[3])
    out = jnp.where(labels == 1, entries[1], out)
    return jnp.where(labels == 2, entries[2], out)


def each(fn, *params):
    return [fn(*(p[k] for p in params)) for k in range(4)]


def edge_columns(field, put):
    for j in range(8):
        put(j, field(j, 0).T[0:8], field(j, 1).T[120:128])


def planes_kernel(u, xm, ym, xym, kept, sem):
    keep = pltpu.make_async_copy(u, kept, sem.at[0])
    keep.start()
    for c in range(3):
        xm[c] = u[c, 0]
        for x in range(32):
            ym[c, x : x + 1, :] = u[c, x, 0:1, :]
        xym[c : c + 1, :] = u[c, 0, 0:1, :]
    keep.wait()


def weight_edges_kernel(weight, odd, labels, near, far):
    start = 24 * (1 - odd[0])

    def step(i, carry):
        near[i] = pick(labels[start + i], weight)
        far[i] = pick(labels[24 - start + i], weight)
        return carry

    lax.fori_loop(0, 8, step, 0, unroll=8)


def columns_kernel(u, labels, nodes):
    lane = lax.broadcasted_iota(jnp.int32, (32, 128), 1)

    def step(x, carry):
        first, last, lab = carry
        for c in range(3):
            at = 40 * c + x
            first = jnp.where(lane == at, pltpu.roll(u[c, x, :, 0:128], at, 1), first)
            last = jnp.where(lane == at, pltpu.roll(u[c, x, :, 128:256], at + 1, 1), last)
        moved = pltpu.roll(labels[x, :, 128:256], x + 1, 1)
        return first, last, jnp.where(lane == x, moved, lab)

    zero = jnp.zeros((32, 128), F32)
    first, last, lab = lax.fori_loop(
        0, 32, step, (zero, zero, jnp.zeros((32, 128), jnp.int32)), unroll=8
    )
    nodes[0:32, :] = first
    nodes[32:64, :] = last
    nodes[64:96, :] = lab.astype(F32)


def combine(d, s, dsh, ssh):
    a = [d[c] + dsh[c] for c in range(3)]
    b = [ssh[c] - s[c] for c in range(3)]
    m = [ssh[c] + s[c] for c in range(3)]
    plus = [a[0], b[1], a[1] + b[0], m[2], b[2] + m[1], a[2] + m[0]]
    minus = [a[0], b[1], a[1] + b[0], m[2], b[2] - m[1], a[2] - m[0]]
    return plus, minus


def root(t):
    return t * lax.rsqrt(jnp.maximum(t, 1e-37))


def response(poisson, weight):
    lead = each(lambda nu, w: 0.1125 * w / (1.0 - 2.0 * nu), poisson, weight)
    shear = each(lambda nu, w: w / (1.0 + nu), poisson, weight)
    return lead, [(0.3 / 48.0) * (f * f) for f in shear]


def respond(applied, law, lab, sums):
    xx, yy, zz = (4.0 * applied[i] + sums[i] for i in range(3))
    xy, yz, xz = (8.0 * applied[i] + sums[j] for i, j in ((5, 3), (3, 4), (4, 5)))
    trace = xx + yy + zz
    p, q = xx - yy, yy - zz
    second = (p * (p + q) + q * q) + 0.75 * (yz * yz + xz * xz + xy * xy)
    lead = pick(lab, law[0]) * trace
    return lead + root(lead * lead + pick(lab, law[1]) * second), second


def strain_kernel(weight, poisson, applied, u, xm, ym, xym, labels, top, second):
    end = lax.broadcasted_iota(jnp.int32, (8, 256), 0) == 7
    inside = lax.broadcasted_iota(jnp.int32, (8, 128), 1) < 127
    law = response(poisson, weight)

    def cells(x, here, there, r_here, r_there):
        below = [
            jnp.broadcast_to(line, (8, 256))
            for c in range(3)
            for line in (r_there[c] - r_here[c], r_there[c] + r_here[c])
        ]
        for k in (3, 2, 1, 0):
            rows = slice(8 * k, 8 * k + 8)
            d, s, dsh, ssh, turned = [], [], [], [], []
            for c in range(3):
                a, b = here(c, rows), there(c, rows)
                d.append(b - a)
                s.append(b + a)
                turned += [pltpu.roll(d[c], 7, 0), pltpu.roll(s[c], 7, 0)]
                dsh.append(jnp.where(end, below[2 * c], turned[2 * c]))
                ssh.append(jnp.where(end, below[2 * c + 1], turned[2 * c + 1]))
            below = turned
            plus, minus = combine(d, s, dsh, ssh)
            shifted = [pltpu.roll(p, 255, 1) for p in plus]
            value, second[x, rows, :] = respond(
                applied,
                law,
                labels[x, rows, :],
                [
                    minus[0] + shifted[0],
                    minus[1] + shifted[1],
                    shifted[3] - minus[3],
                    minus[2] + shifted[2],
                    minus[4] + shifted[4],
                    minus[5] + shifted[5],
                ],
            )
            top[x, rows, 0:128] = value[:, 0:128]
            top[x, rows, 128:256] = jnp.where(inside, value[:, 128:256], 0.0)

    def step(x, carry):
        cells(
            x,
            lambda c, rows: u[c, x, rows, :],
            lambda c, rows: u[c, x + 1, rows, :],
            [ym[c, pl.ds(x, 1), :] for c in range(3)],
            [ym[c, pl.ds(x + 1, 1), :] for c in range(3)],
        )
        return carry

    lax.fori_loop(0, 31, step, 0)
    cells(
        31,
        lambda c, rows: u[c, 31, rows, :],
        lambda c, rows: xm[c, rows, :],
        [ym[c, 31:32, :] for c in range(3)],
        [xym[c : c + 1, :] for c in range(3)],
    )


def columns_out(field, out, first):
    def put(j, low, high):
        at = first + 16 * j
        out[at : at + 16, :] = jnp.concatenate([high, low], axis=0)

    edge_columns(
        lambda j, t: field[4 * j : 4 * j + 4, :, 128 * t : 128 * t + 128].reshape(128, 128), put
    )


def zpack_kernel(top, nodes, xm, ym, xym, out):
    columns_out(top, out, 0)
    lane = lax.broadcasted_iota(jnp.int32, (32, 128), 1)
    lane1 = lax.broadcasted_iota(jnp.int32, (8, 128), 1)
    pad = jnp.zeros((96, 128), F32)
    for t in range(2):
        body = nodes[32 * t : 32 * t + 32, :]
        edge = jnp.zeros((8, 128), F32)
        for c in range(3):
            at = 40 * c + 32
            lanes = slice(128 * t, 128 * t + 128)
            body = jnp.where(lane == at, pltpu.roll(xm[c, :, lanes], (at + t) % 128, 1), body)
            turned = jnp.concatenate([ym[c, :, lanes], pad], axis=0).T
            line = turned[127:128] if t else turned[0:1]
            line = pltpu.roll(jnp.broadcast_to(line, (8, 128)), 40 * c, 1)
            corner = pltpu.roll(jnp.broadcast_to(xym[c : c + 1, lanes], (8, 128)), (at + t) % 128, 1)
            edge = jnp.where((lane1 >= 40 * c) & (lane1 < at), line, edge)
            edge = jnp.where(lane1 == at, corner, edge)
        out[128 + 40 * t : 160 + 40 * t, :] = body
        out[160 + 40 * t : 168 + 40 * t, :] = edge
    out[208:240, :] = nodes[64:96, :]


def column_cells(applied, law, lower, upper, lab):
    parts = []
    for n in (lower, upper):
        nx = pltpu.roll(n, 127, 1)
        d, s = nx - n, nx + n
        dsh, ssh = pltpu.roll(d, 39, 0), pltpu.roll(s, 39, 0)
        parts.append((d + dsh, ssh - s, ssh + s))
    gx = (parts[0][0] + parts[1][0])[0:32]
    gy = (parts[0][1] + parts[1][1])[0:32]
    gz = (parts[1][2] - parts[0][2])[0:32]
    gx = [gx, pltpu.roll(gx, 88, 1), pltpu.roll(gx, 48, 1)]
    gy = [gy, pltpu.roll(gy, 88, 1), pltpu.roll(gy, 48, 1)]
    gz = [gz, pltpu.roll(gz, 88, 1), pltpu.roll(gz, 48, 1)]
    return respond(
        applied,
        law,
        lab.astype(jnp.int32),
        [gx[0], gy[1], gz[2], gx[1] + gy[0], gy[2] + gz[1], gx[2] + gz[0]],
    )


def blocks_of(cells, scratch):
    keep = lax.broadcasted_iota(jnp.int32, (32, 128), 1) < 32
    padded = jnp.concatenate([jnp.where(keep, cells, 0.0), jnp.zeros((96, 128), F32)], axis=0)
    scratch[...] = padded.T[0:32]
    total = scratch[pl.ds(0, 8, stride=4), :]
    for i in range(1, 4):
        total = total + pltpu.roll(scratch[pl.ds(i, 8, stride=4), :], 32 * i, 1)
    return total


def z_local_kernel(field, gz, out):
    for j in range(8):
        hi, lo = split(field[4 * j : 4 * j + 4].reshape(128, 256))
        part = mxu(hi, gz[0], ((1,), (0,))) + mxu(lo, gz[0], ((1,), (0,)))
        part = part + mxu(hi, gz[1], ((1,), (0,)))
        out[4 * j : 4 * j + 4] = part.reshape(4, 32, 256)


def z_halo(local, halo, gh, out, before=None, last=None):
    for j in range(8):
        lines = halo[16 * j : 16 * j + 16, :]
        if before is None:
            rows = [lines, jnp.zeros((8, 128), F32)]
        else:
            rows = [lines[0:7], before[j : j + 1], lines[8:16], last[j : j + 1], jnp.zeros((7, 128), F32)]
        chi, clo = split(jnp.concatenate(rows, axis=0).T)
        c = jnp.concatenate([chi, clo, chi], axis=1)
        part = mxu(c, gh[...], ((1,), (0,))).reshape(4, 32, 256)
        out[4 * j : 4 * j + 4] = local[4 * j : 4 * j + 4] + part


def top_z_kernel(weight, poisson, applied, odd, local, mine, peer, gh, out, near, far, second_last, scratch):
    law = response(poisson, weight)
    last, second_last[...] = column_cells(
        applied, law, mine[168:208, :], peer[128:168, :], mine[208:240, :]
    )
    before, _ = column_cells(applied, law, peer[168:208, :], mine[128:168, :], peer[208:240, :])
    last, before = blocks_of(last, scratch), blocks_of(before, scratch)
    z_halo(local, peer, gh, out, before, last)
    y_edges(odd, out, near, far)


def weights_z_kernel(local, peer, gh, inverse):
    z_halo(local, peer, gh, inverse)
    inverse[...] = 1.0 / inverse[...]


def y_edges(odd, out, near, far):
    start = pl.multiple_of(24 * (1 - odd[1]), 8)
    near[...] = out[:, pl.ds(start, 8), :]
    far[...] = out[:, pl.ds(pl.multiple_of(24 - start, 8), 8), :]


def smooth_x(odd, cell, r_near, r_far, out):
    is_odd = odd[0] == 1
    table = taps()

    def step(k, carry):
        rows = pl.ds(pl.multiple_of((k // 2) * 8, 8), 8)
        lanes = pl.ds(pl.multiple_of((k % 2) * 128, 128), 128)
        low, high = [], []
        for i in range(8):
            a, b = r_near[i, rows, lanes], r_far[i, rows, lanes]
            low.append(jnp.where(is_odd, a, b))
            high.append(jnp.where(is_odd, b, a))
        cells = low + [cell(i, rows, lanes) for i in range(32)] + high
        for i in range(32):
            total = table[8] * cells[i + 8]
            for s in range(1, 9):
                total = total + table[8 + s] * (cells[i + 8 - s] + cells[i + 8 + s])
            out[i, rows, lanes] = total
        return carry

    lax.fori_loop(0, 8, step, 0)


def weights_x_kernel(weight, odd, labels, r_near, r_far, out, near, far):
    smooth_x(odd, lambda *at: pick(labels[at], weight), r_near, r_far, out)
    y_edges(odd, out, near, far)


def smooth_y(x, is_odd, field, r_near, r_far, gy):
    a, b = r_near[x], r_far[x]
    cells = jnp.concatenate([jnp.where(is_odd, a, b), field[x], jnp.where(is_odd, b, a)], axis=0)
    hi, lo = split(cells)
    return mxu(gy[...], jnp.concatenate([hi, lo, hi], axis=0), ((1,), (0,)))


def smooth_all_y(odd, field, r_near, r_far, gy, out):
    is_odd = odd[1] == 1

    def step(x, carry):
        out[x] = smooth_y(x, is_odd, field, r_near, r_far, gy)
        return carry

    lax.fori_loop(0, 32, step, 0, unroll=8)


def weights_y_kernel(odd, field, r_near, r_far, gy, gz, out, cols):
    smooth_all_y(odd, field, r_near, r_far, gy, out)
    columns_out(out, cols, 0)
    z_local_kernel(out, gz, out)


def top_y_far_kernel(odd, field, r_near, r_far, gy, far):
    is_odd, first = odd[1] == 1, 24 * odd[0]

    def step(i, carry):
        far[i] = smooth_y(first + i, is_odd, field, r_near, r_far, gy)
        return carry

    lax.fori_loop(0, 8, step, 0, unroll=8)


def top_y_kernel(odd, field, r_near, r_far, gy, far, out, near):
    is_odd, first = odd[1] == 1, 8 * (1 - odd[0])

    def step(i, carry):
        out[first + i] = smooth_y(first + i, is_odd, field, r_near, r_far, gy)
        return carry

    lax.fori_loop(0, 24, step, 0, unroll=8)
    out[pl.ds(24 * odd[0], 8)] = far[...]
    near[...] = out[pl.ds(24 * (1 - odd[0]), 8)]


def phases_kernel(
    modulus, poisson, threshold, ductility, brittleness,
    labels, second, second_last, stress, start, lost, ductile, brittle,
):
    lane = lax.broadcasted_iota(jnp.int32, (32, 128), 1)
    stiff = each(lambda e, nu: math.sqrt(3.0 / 48.0) * e / (1.0 + nu), modulus, poisson)
    gone = each(lambda k, a: k * (1.0 - a), threshold, ductility)
    rate = each(lambda b: b * math.log2(math.e), brittleness)

    def step(x, carry):
        lab = labels[x]
        moved = pltpu.roll(second_last[...], 127 - x, 1)
        end = jnp.where(lane == 127, moved, second[x, :, 128:256])
        whole = jnp.concatenate([second[x, :, 0:128], end], axis=1)
        stress[x] = pick(lab, stiff) * root(whole)
        start[x] = pick(lab, threshold)
        lost[x] = pick(lab, gone)
        ductile[x] = pick(lab, ductility)
        brittle[x] = pick(lab, rate)
        return carry

    lax.fori_loop(0, 32, step, 0, unroll=4)


def finish_cells(averaged, history, stress, start, lost, ductile, brittle):
    kappa = jnp.maximum(history, averaged)
    grown = 1.0 - lost / kappa - ductile * jnp.exp2(brittle * (start - kappa))
    harm = jnp.where(kappa > start, grown, 0.0)
    return harm, (1.0 - harm) * stress


def finish_planes(window, count, first, inverse, fields, d_buf, m_buf, damage, mises, sem):
    g = taps()

    def step(k):
        rows = pl.ds(pl.multiple_of((k // 2) * 8, 8), 8)
        lanes = pl.ds(pl.multiple_of((k % 2) * 128, 128), 128)
        cells = [window(w, rows, lanes) for w in range(count + 16)]
        for i in range(count):
            total = g[8] * cells[i + 8]
            for s in range(1, 9):
                total = total + g[8 + s] * (cells[i + 8 - s] + cells[i + 8 + s])
            at = (first + i, rows, lanes)
            harm, von_mises = finish_cells(total * inverse[at], *(f[at] for f in fields))
            d_buf[i, rows, lanes] = harm
            m_buf[i, rows, lanes] = von_mises

    def copies(t):
        rows = slice(8 * t, 8 * t + 8)
        place = (pl.ds(first, count), rows)
        return [
            pltpu.make_async_copy(d_buf.at[:, rows], damage.at[place], sem.at[0, t]),
            pltpu.make_async_copy(m_buf.at[:, rows], mises.at[place], sem.at[1, t]),
        ]

    for t in range(4):

        def half(k, carry, t=t):
            step(2 * t + k)
            return carry

        lax.fori_loop(0, 2, half, 0)
        for copy in copies(t):
            copy.start()
    for t in range(4):
        for copy in copies(t):
            copy.wait()


def finish_most_kernel(odd, field, near, inverse, *refs):
    is_odd, shift = odd[0] == 1, 8 * odd[0]

    def window(w, rows, lanes):
        if w < 8:
            return jnp.where(is_odd, near[w, rows, lanes], field[w, rows, lanes])
        if w < 32:
            return field[w - shift, rows, lanes]
        return jnp.where(is_odd, field[w - 8, rows, lanes], near[w - 32, rows, lanes])

    first = 8 - shift
    damage, mises, d_buf, m_buf, sem = refs[6:]
    finish_planes(window, 24, first, inverse, refs[:6], d_buf, m_buf, damage, mises, sem)


def finish_rest_kernel(odd, field, far, inverse, *refs):
    is_odd, shift = odd[0] == 1, 8 * odd[0]

    def window(w, rows, lanes):
        if w < 8:
            return jnp.where(is_odd, field[16 + w, rows, lanes], far[w, rows, lanes])
        if w < 16:
            return field[w - 8 + 3 * shift, rows, lanes]
        return jnp.where(is_odd, far[w - 16, rows, lanes], field[w - 8, rows, lanes])

    first = 3 * shift
    damage, mises, d_buf, m_buf, sem = refs[8:]
    finish_planes(window, 8, first, inverse, refs[:6], d_buf, m_buf, damage, mises, sem)


def shards(
    displacement,
    applied_strain,
    labels,
    history,
    modulus,
    poisson,
    threshold,
    ductility,
    brittleness,
    weight,
):
    gz = jnp.stack([jnp.asarray(m) for m in split_const(band(256, 256, 0).T)])
    low, high = band(256, 8, -8).T, band(256, 8, 256).T
    own = band(256, 256, 0).T[255:256]
    h_hi, h_lo = split_const(np.concatenate([low, high, own, np.zeros((7, 256))], axis=0))
    gh = jnp.asarray(np.concatenate([h_hi, h_hi, h_lo], axis=0))
    y_hi, y_lo = split_const(band(32, 48, -8))
    gy = jnp.asarray(np.concatenate([y_hi, y_hi, y_lo], axis=1))

    field3, edge_x, edge_y = (32, 32, 256), (8, 32, 256), (32, 8, 256)
    hbm, vmem, dma = pltpu.HBM, pltpu.VMEM, pltpu.SemaphoreType.DMA
    xm, ym, xym, displacement = call(
        planes_kernel, [(3, 32, 256), (3, 32, 256), (8, 256), displacement.shape], scratch=[dma((1,))],
    )(displacement)
    x_token = xm
    xm = shift_route(xm, ("gx",), (-1,))
    ym = shift_route(ym, ("gy",), (-1,))
    xym = shift_route(xym, ("gx", "gy"), (-1, -1))
    (nodes,) = call(columns_kernel, [(96, 128)], n_in=2, after=(x_token,))(displacement, labels)
    near, far = call(weight_edges_kernel, [edge_x, edge_x], n_in=2, smem=(0,), odd=1, after=(nodes,))(weight, labels)
    w_near = swap_route(near, "gx", 0)
    w_far = swap_route(far, "gx", 1)
    top, second = call(strain_kernel, [field3, field3], n_in=8, smem=(0, 1, 2))(
        weight, poisson, applied_strain, displacement, xm, ym, xym, labels
    )
    (mine,) = call(zpack_kernel, [(240, 128)], n_in=5)(top, nodes, xm, ym, xym)
    peer = shift_route(mine, ("gz",), (1,))
    weights, near, far = call(
        weights_x_kernel, [field3, edge_y, edge_y], n_in=4, smem=(0,), odd=1, after=(mine,)
    )(weight, labels, w_near, w_far)
    w_near = swap_route(near, "gy", 0)
    w_far = swap_route(far, "gy", 1)
    (local,) = call(z_local_kernel, [field3], n_in=2, after=(near,))(top, gz)
    top, near, far, second_last = call(
        top_z_kernel, [field3, edge_y, edge_y, (32, 128)], scratch=[vmem((32, 128), F32)], n_in=7, smem=(0, 1, 2), odd=3
    )(weight, poisson, applied_strain, local, mine, peer, gh)
    t_near = swap_route(near, "gy", 0)
    t_far = swap_route(far, "gy", 1)
    phases = call(
        phases_kernel, [field3] * 5, n_in=8, smem=range(5), after=(near,)
    )(modulus, poisson, threshold, ductility, brittleness, labels, second, second_last)
    weights, cols = call(
        weights_y_kernel, [field3, (128, 128)], n_in=5, odd=0, after=(phases[0],)
    )(weights, w_near, w_far, gy, gz)
    z_token = cols
    cols = shift_route(cols, ("gz",), (1,))
    (far,) = call(top_y_far_kernel, [edge_x], n_in=4, odd=0, after=(z_token,))(top, t_near, t_far, gy)
    top, near = call(top_y_kernel, [field3, edge_x], n_in=5, odd=0)(
        top, t_near, t_far, gy, far
    )
    (inverse,) = call(weights_z_kernel, [field3], n_in=3, after=(near,))(weights, cols, gh)
    far = swap_route(far, "gx", 1)
    near = swap_route(near, "gx", 0)
    outs = [field3, field3]
    fields = (inverse, history, *phases)
    damage, mises = call(
        finish_most_kernel, outs, n_in=9, odd=0, out_spaces=[hbm, hbm],
        scratch=[vmem((24, 32, 256), F32), vmem((24, 32, 256), F32), dma((2, 4))],
    )(top, near, *fields)
    return call(
        finish_rest_kernel, outs, odd=0, out_spaces=[hbm, hbm],
        spaces=[None] * 9 + [hbm, hbm], aliases={9: 0, 10: 1},
        scratch=[vmem((8, 32, 256), F32), vmem((8, 32, 256), F32), dma((2, 4))],
    )(top, far, *fields, damage, mises)


def solution(mesh):
    cells = P("gx", "gy", "gz")
    placed = (P(None, "gx", "gy", "gz"), P(), cells, cells, P(), P(), P(), P(), P(), P())

    def body(*args):
        return tuple(shards(*args))

    return jax.shard_map(
        body, mesh=mesh, in_specs=placed, out_specs=(cells, cells), check_vma=False
    )
```
